256 devices in a mesh: dp: 32 (over z, x_hi, core), seq: 8 (over y, x_lo).
Axes of the slice: x: 4 (x_hi: 2, x_lo: 2; x = x_hi * 2 + x_lo), y: 4, z: 8, core: 2. Of those that a mesh axis runs over, the one named last changes fastest.
Arguments:
- grad_out: bfloat16 [32, 1024, 6144], P('dp', 'seq'), may hold values from -6 to 6
- queries: bfloat16 [32, 1024, 3072], P('dp', 'seq'), may hold values from -40 to 40
- keys: bfloat16 [32, 1024, 3072], P('dp', 'seq'), may hold values from -12 to 12
- values: bfloat16 [32, 1024, 3072], P('dp', 'seq'), may hold values from -6 to 6
- out_weight: bfloat16 [6144, 3072], P('dp', 'seq'), may hold values from -0.109375 to 0.109375
Outputs:
- query_grad: bfloat16 [32, 1024, 3072], P('dp', 'seq')
- key_grad: bfloat16 [32, 1024, 3072], P('dp', 'seq')
- value_grad: bfloat16 [32, 1024, 3072], P('dp', 'seq')
- weight_grad: float32 [6144, 3072], P('dp', 'seq')
The draws below stay inside these ranges and needn't reach their ends.
All inputs are finite; a program needn't handle non-finite values.
Results may differ from the reference program's by a relative error of at most 0.03.
Values may be sent and summed in bfloat16 or wider, within the bound.
A program may use at most 128 MiB of HBM per device.

```python
import math
import jax
import jax.numpy as jnp
from jax import lax

D = 6144
HEADS = 24
HEAD_DIM = 128
LEN = 1024
BATCH = 32


def query_key_pair(key):
    base = jax.random.fold_in(key, 31)
    first, second = jax.random.split(base, 2)
    array_shape = (BATCH, LEN, HEADS * HEAD_DIM)
    key_rows = jax.random.truncated_normal(first, -4.0, 4.0, array_shape, jnp.float32)
    query_rows = 2.5 * jax.random.truncated_normal(second, -4.0, 4.0, array_shape, jnp.float32)
    return (query_rows, key_rows)


def draw_queries(key, part):
    return query_key_pair(key)[0].astype(jnp.bfloat16)


def draw_keys(key, part):
    return query_key_pair(key)[1].astype(jnp.bfloat16)


def spiked(array, key, source, target, shards_of, factor):
    def block_of(axis_at):
        return (jnp.arange(array.shape[axis_at]) // (array.shape[axis_at] // shards_of)).reshape((-1,) + (1,) * (array.ndim - 1 - axis_at))

    near = jax.random.permutation(key, shards_of)[block_of(target)]
    second = (block_of(target) + shards_of // 2) % shards_of
    return jnp.where((block_of(source) == near) | (block_of(source) == second), factor * array, array)


def shard_levels(own_key, shape, cuts, low, top_value):
    factor_of, own = 1.0, jax.random.fold_in(own_key, 6)
    for axis_at, parts in cuts:
        draws = jnp.exp(jax.random.uniform(jax.random.fold_in(own, axis_at), (parts,), jnp.float32, low / len(cuts), top_value / len(cuts)))
        factor_of = factor_of * jnp.repeat(draws, shape[axis_at] // parts).reshape([-1 if axis == axis_at else 1 for axis in range(len(shape))])
    return factor_of


def gaussian(own_key, dims, scale, bound, cuts=(), dtype=jnp.bfloat16):
    values = scale * jax.random.normal(own_key, dims, jnp.float32)
    if cuts:
        values = values * shard_levels(own_key, dims, cuts, -0.22, 0.18)
    return jnp.clip(values, -bound, bound).astype(dtype)


def bell_draw_with(own_key, shape, scale, limit, pieces, heavy, dtype=jnp.bfloat16):
    entries = scale * jax.random.normal(own_key, shape, jnp.float32)
    if pieces:
        entries = entries * shard_levels(own_key, shape, pieces, -0.22, 0.18)
    return jnp.clip(spiked(entries, jax.random.fold_in(own_key, 3), *heavy), -limit, limit).astype(dtype)


def setup_inputs(seed: int = 0) -> dict:
    arg_keys = jax.random.split(jax.random.key(seed), 6)
    return {
        "grad_out": bell_draw_with(arg_keys[0], (BATCH, LEN, D), 1.0, 6.0, ((0, 32), (1, 8)), (0, 2, 32, 2.75)),
        "queries": draw_queries(jax.random.fold_in(arg_keys[5], 71), 0),
        "keys": draw_keys(jax.random.fold_in(arg_keys[5], 71), 0),
        "values": gaussian(arg_keys[3], (BATCH, LEN, HEADS * HEAD_DIM), 1.0, 6.0, ((0, 32), (1, 8))),
        "out_weight": gaussian(arg_keys[4], (D, HEADS * HEAD_DIM), (HEADS * HEAD_DIM) ** -0.5, 0.109375, ((0, 32), (1, 8))),
    }


def sequence_grads(grad_rows, query_rows, key_rows, value_rows, out_weight):
    d_attn = jnp.dot(grad_rows, out_weight, preferred_element_type=jnp.float32).astype(jnp.bfloat16)
    head_shape = (LEN, HEADS, HEAD_DIM)
    query_heads = query_rows.reshape(head_shape).astype(jnp.float32)
    key_heads = key_rows.reshape(head_shape).astype(jnp.float32)
    value_heads = value_rows.reshape(head_shape).astype(jnp.float32)
    grad_heads = d_attn.reshape(head_shape).astype(jnp.float32)
    inverse_root = 1.0 / math.sqrt(HEAD_DIM)
    scores = jnp.einsum('qhd,khd->hqk', query_heads, key_heads) * inverse_root
    largest = lax.optimization_barrier(jnp.max(scores, axis=-1, keepdims=True))
    raised = jnp.exp(scores - largest)
    probabilities = raised / lax.optimization_barrier(jnp.sum(raised, axis=-1, keepdims=True))
    probs_low = probabilities.astype(jnp.bfloat16).astype(jnp.float32)
    attended = jnp.einsum('hqk,khd->qhd', probs_low, value_heads).astype(jnp.bfloat16)
    row_delta = lax.optimization_barrier(jnp.sum(grad_heads * attended.astype(jnp.float32), axis=-1))
    d_probs = jnp.einsum('qhd,khd->hqk', grad_heads, value_heads)
    d_scores = probabilities * (d_probs - jnp.transpose(row_delta)[:, :, None])
    scores_low = d_scores.astype(jnp.bfloat16).astype(jnp.float32)
    value_grad = jnp.einsum('hqk,qhd->khd', probs_low, grad_heads).astype(jnp.bfloat16)
    query_grad = (jnp.einsum('hqk,khd->qhd', scores_low, key_heads) * inverse_root).astype(jnp.bfloat16)
    key_grad = (jnp.einsum('hqk,qhd->khd', scores_low, query_heads) * inverse_root).astype(jnp.bfloat16)
    features = HEADS * HEAD_DIM
    return (query_grad.reshape(LEN, features), key_grad.reshape(LEN, features), value_grad.reshape(LEN, features), attended.reshape(LEN, features))

def reference(grad_out, queries, keys, values, out_weight):

    def per_sequence(inputs):
        return sequence_grads(inputs[0], inputs[1], inputs[2], inputs[3], out_weight)
    query_grad, key_grad, value_grad, attended = lax.map(per_sequence, (grad_out, queries, keys, values))
    flat_grad = grad_out.reshape(BATCH * LEN, D)
    flat_attended = attended.reshape(BATCH * LEN, HEADS * HEAD_DIM)
    weight_grad = jnp.dot(flat_grad.T, flat_attended, preferred_element_type=jnp.float32) / math.sqrt(BATCH * LEN)
    return (query_grad, key_grad, value_grad, weight_grad)
```

```python
import math

import jax
import jax.numpy as jnp
from jax import lax
from jax.experimental import pallas as pl
from jax.experimental.pallas import tpu as pltpu
from jax.sharding import PartitionSpec as P

HEAD_DIM = 128
MESH = pl.DeviceIdType.MESH
F32 = jnp.float32
BF16 = jnp.bfloat16
NZ, NY = 8, 4
NT = (((1,), (1,)), ((), ()))
TN = (((0,), (0,)), ((), ()))


def dot(a, b):
    return jnp.dot(a, b, preferred_element_type=F32)


def make_kernel(tokens, model, wide, rows, cols, clips):
    heads = cols // HEAD_DIM
    length = tokens * 8
    half = length // 2
    strip = 2 * rows
    pair = 2 * cols
    deep = NZ * strip
    inverse_root = 1.0 / math.sqrt(HEAD_DIM)
    power = inverse_root * math.log2(math.e)
    token_scale = 1.0 / math.sqrt(clips * length)
    block = 256
    blocks = length // block

    def kernel(
        g_in, q_in, k_in, v_in, w_in,
        dq_out, dk_out, dv_out, wg_out,
        gb, wb, qb, kb, vb, pt, dsb, kt, vt, ot, att, acat, dob, dsend, dacc,
        pb, rc, rr, fx, xr, dqb, dkb, dvb,
        loc, wx_s, wx_r, wz_s, wz_r, wc_s, wc_r, qkv_s, qkv_r, g_s, g_r,
        ex_s, ex_r, pc_s, pc_r, rr_s, rr_r, x_s, x_r, gr_s, gr_r,
    ):
        dp = lax.axis_index("dp")
        seq = lax.axis_index("seq")
        z, xh, c = dp // 4, (dp // 2) % 2, dp % 2
        y, xl = seq // 2, seq % 2

        def seq_peer(dy, b):
            return {"dp": dp, "seq": ((y + dy) % NY) * 2 + (xl + b) % 2}

        def x_peer(a, b):
            return {"dp": z * 4 + ((xh + a) % 2) * 2 + c, "seq": y * 2 + (xl + b) % 2}

        def z_peer(dz):
            return {"dp": ((z + dz + NZ) % NZ) * 4 + xh * 2 + c, "seq": seq}

        core_peer = {"dp": z * 4 + xh * 2 + (1 - c), "seq": seq}
        seq_offsets = [(dy, b) for dy in range(NY) for b in range(2) if dy or b]
        x_offsets = [(0, 1), (1, 1), (1, 0)]

        def remote(src, dst, send, recv, device):
            copy = pltpu.make_async_remote_copy(
                src_ref=src, dst_ref=dst, send_sem=send, recv_sem=recv,
                device_id=device, device_id_type=MESH,
            )
            copy.start()
            return copy

        barrier = pltpu.get_barrier_semaphore()
        partners = [seq_peer(*o) for o in seq_offsets] + [core_peer, z_peer(1), z_peer(-1)]
        partners += [x_peer(1, 0), x_peer(1, 1)]
        for device in partners:
            pl.semaphore_signal(barrier, inc=1, device_id=device, device_id_type=MESH)

        def w_rows(zz, cc):
            return pl.ds(pl.multiple_of(zz * strip + cc * rows, 64), rows)

        def col(i, width):
            return pl.ds(pl.multiple_of(i * width, 128), width)

        own_rows = pl.ds(pl.multiple_of(xl * half + y * tokens, 128), tokens)
        y_rows = pl.ds(pl.multiple_of(y * tokens, 128), tokens)
        local = [
            pltpu.make_async_copy(
                w_in, wb.at[xh, w_rows(z, c), col(xl, cols)], loc.at[0]
            )
        ]
        for t, (src, dst) in enumerate(((q_in, qb), (k_in, kb), (v_in, vb))):
            local.append(
                pltpu.make_async_copy(src.at[:, col(seq, cols)], dst.at[own_rows, :], loc.at[1 + t])
            )
        for s in range(2):
            for zz in range(NZ):
                local.append(
                    pltpu.make_async_copy(
                        g_in.at[:, pl.ds((2 * zz + s) * strip, strip)],
                        gb.at[s, y_rows, pl.ds(zz * strip, strip)],
                        loc.at[4 + s * NZ + zz],
                    )
                )
        for copy in local:
            copy.start()
        pl.semaphore_wait(barrier, len(partners))

        wx = [
            remote(
                w_in, wb.at[xh, w_rows(z, c), col(xl, cols)], wx_s.at[i], wx_r.at[i], x_peer(a, b)
            )
            for i, (a, b) in enumerate(x_offsets)
        ]
        qkv = []
        for i, (dy, b) in enumerate(seq_offsets):
            device = seq_peer(dy, b)
            for t, (src, dst) in enumerate(((q_in, qb), (k_in, kb), (v_in, vb))):
                qkv.append(
                    remote(
                        src.at[:, col(device["seq"], cols)], dst.at[own_rows, :],
                        qkv_s.at[i, t], qkv_r.at[i, t], device,
                    )
                )
        for copy in local:
            copy.wait()
        for copy in wx:
            copy.wait_recv()

        wz = {}
        wc = []

        def w_block(s, zz, cc):
            return wb.at[s, w_rows(zz, cc), :]

        def w_core(s, zz, slot):
            wc.append(
                remote(w_block(s, zz, c), w_block(s, zz, c), wc_s.at[s, slot], wc_r.at[s, slot], core_peer)
            )

        def w_send(d, s, j):
            zz = (z - j + NZ) % NZ if d == 0 else (z + j) % NZ
            ref = w_block(s, zz, c)
            wz[d, s, j] = remote(ref, ref, wz_s.at[d, s, j], wz_r.at[d, s, j], z_peer(1 if d == 0 else -1))

        def w_steps(d, s):
            return 4 if d == s else 3

        for s in range(2):
            for d in range(2):
                w_send(d, s, 0)
        for s in range(2):
            w_core(s, z, 0)
        for j in range(4):
            for s in range(2):
                for d in range(2):
                    if j < w_steps(d, s):
                        wz[d, s, j].wait_recv()
                        if j + 1 < w_steps(d, s):
                            w_send(d, s, j + 1)
                        zz = (z - 1 - j + NZ) % NZ if d == 0 else (z + 1 + j) % NZ
                        w_core(s, zz, 1 + 2 * j + d if j < 3 else 7)

        g = {}
        for s in range(2):
            for dy in (1, 3, 2):
                for zz in range(NZ):
                    g[s, dy, zz] = remote(
                        g_in.at[:, pl.ds((2 * zz + s) * strip, strip)],
                        gb.at[s, y_rows, pl.ds(zz * strip, strip)],
                        g_s.at[s, dy - 1, zz], g_r.at[s, dy - 1, zz], seq_peer(dy, 0),
                    )

        for copy in qkv:
            copy.wait_recv()

        for h in range(heads):
            hc = pl.ds(h * HEAD_DIM, HEAD_DIM)
            kt[h] = jnp.transpose(kb[:, hc].astype(F32)).astype(BF16)
            vt[h] = jnp.transpose(vb[:, hc].astype(F32)).astype(BF16)

            @pl.loop(0, blocks)
            def _(i):
                at = pl.ds(pl.multiple_of(i * block, block), block)
                scores = lax.dot_general(kb[:, hc], qb[at, hc], NT, preferred_element_type=F32)
                largest = jnp.max(scores, axis=0, keepdims=True)
                raised = jnp.exp2((scores - largest) * power)
                total = jnp.sum(raised, axis=0, keepdims=True)
                low = (raised * (1.0 / total)).astype(BF16)
                pt[h, :, at] = low
                out = dot(vt[h], low).astype(BF16)
                ot[h, :, at] = out
                att[at, hc] = jnp.transpose(out.astype(F32)).astype(BF16)

        mine = pl.ds(pl.multiple_of(xl * half, 128), half)
        theirs = pl.ds(pl.multiple_of((1 - xl) * half, 128), half)
        x_partner = seq_peer(0, 1)
        att_copy = remote(
            att.at[theirs, :], acat.at[:, col(xl, cols)], ex_s.at[0], ex_r.at[0], x_partner
        )
        acat[:, col(xl, cols)] = att[mine, :]
        att_copy.wait_recv()
        for copy in wc:
            copy.wait_recv()

        def project(s):
            chunk = deep // 4

            @pl.loop(0, 4)
            def _(i):
                at = pl.ds(pl.multiple_of(i * chunk, 128), chunk)
                part = dot(gb[s, :, at], wb[s, at, :])
                if s == 0:
                    dacc[...] = jnp.where(i == 0, part, dacc[...] + part)
                else:
                    dacc[...] += part

        def weight_terms(s):
            @pl.loop(0, NZ)
            def _(i):
                at = pl.ds(pl.multiple_of(i * strip, 128), strip)
                part = lax.dot_general(gb[s, :, at], acat[...], TN, preferred_element_type=F32)
                pb[s, i] = (part * token_scale).astype(BF16).reshape(2, rows, pair)

        def core_terms(s):
            return remote(pb.at[s, :, 1 - c], rc.at[s], pc_s.at[s], pc_r.at[s], core_peer)

        ring = {}

        def ring_value(s, d, k, zd):
            dc = pl.ds(d * cols, cols)
            value = pb[s, zd, c, :, dc].astype(F32) + rc[s, zd, :, dc].astype(F32)
            if k > 0:
                value = value + rr[s, d, k - 1].astype(F32)
            return value

        def ring_send(s, k):
            for d in range(2):
                if k > 0:
                    ring[s, d, k - 1].wait_recv()
                zd = (z - 1 - k + NZ) % NZ if d == 0 else (z + 1 + k) % NZ
                dc = pl.ds(d * cols, cols)
                value = ring_value(s, d, k, zd).astype(BF16)
                rc[s, zd, :, dc] = value
                ring[s, d, k] = remote(
                    rc.at[s, zd, :, dc], rr.at[s, d, k], rr_s.at[s, d, k], rr_r.at[s, d, k],
                    z_peer(1 if d == 0 else -1),
                )

        def ring_last(s):
            for d in range(2):
                ring[s, d, NZ - 2].wait_recv()
                fx[s, d] = ring_value(s, d, NZ - 1, z).astype(BF16)

        def wait_g(s):
            for dy in (1, 3, 2):
                for zz in range(NZ):
                    g[s, dy, zz].wait_recv()

        wait_g(0)
        weight_terms(0)
        pc = [core_terms(0)]
        project(0)
        pc[0].wait_recv()
        for k in range(4):
            ring_send(0, k)
        wait_g(1)
        project(1)
        dob[mine, :] = dacc[:, col(xl, cols)].astype(BF16)
        dsend[...] = dacc[:, col(1 - xl, cols)].astype(BF16)
        d_copy = remote(dsend, dob.at[mine, :], ex_s.at[1], ex_r.at[1], x_partner)
        weight_terms(1)
        pc.append(core_terms(1))
        ring_send(0, 4)
        pc[1].wait_recv()
        ring_send(1, 0)
        d_copy.wait_recv()

        grads = []

        def backward(h):
            hc = pl.ds(h * HEAD_DIM, HEAD_DIM)

            @pl.loop(0, blocks)
            def _(i):
                at = pl.ds(pl.multiple_of(i * block, block), block)
                rows_d = dob[at, hc]
                d_probs = lax.dot_general(vb[:, hc], rows_d, NT, preferred_element_type=F32)
                delta = jnp.sum(
                    jnp.transpose(rows_d.astype(F32)) * ot[h, :, at].astype(F32),
                    axis=0, keepdims=True,
                )
                low = (pt[h, :, at].astype(F32) * (d_probs - delta)).astype(BF16)
                dsb[:, at] = low
                dqb[at, hc] = jnp.transpose(dot(kt[h], low) * inverse_root).astype(BF16)

            @pl.loop(0, blocks)
            def _(i):
                at = pl.ds(pl.multiple_of(i * block, block), block)
                dvb[at, hc] = dot(pt[h, at, :], dob[:, hc]).astype(BF16)
                dkb[at, hc] = (dot(dsb[at, :], qb[:, hc]) * inverse_root).astype(BF16)

            out_cols = pl.ds(pl.multiple_of(seq * cols + h * HEAD_DIM, 128), HEAD_DIM)
            for t, (src, dst) in enumerate(((dqb, dq_out), (dkb, dk_out), (dvb, dv_out))):
                for i, (dy, b) in enumerate(seq_offsets):
                    token_rows = ((xl + b) % 2) * half + ((y + dy) % NY) * tokens
                    grads.append(
                        remote(
                            src.at[pl.ds(pl.multiple_of(token_rows, 128), tokens), hc],
                            dst.at[:, out_cols],
                            gr_s.at[h, i, t], gr_r.at[h, i, t], seq_peer(dy, b),
                        )
                    )
                copy = pltpu.make_async_copy(
                    src.at[own_rows, hc], dst.at[:, out_cols], loc.at[20 + h * 3 + t]
                )
                copy.start()
                grads.append(copy)

        backward(0)
        ring_send(0, 5)
        ring_send(1, 1)
        backward(1)
        ring_send(0, 6)
        ring_send(1, 2)
        backward(2)
        ring_last(0)
        for k in range(3, NZ - 1):
            ring_send(1, k)
        ring_last(1)

        xs = [
            remote(
                fx.at[(xh + a) % 2, (xl + b) % 2], xr.at[i], x_s.at[i], x_r.at[i], x_peer(a, b)
            )
            for i, (a, b) in enumerate(x_offsets)
        ]
        for copy in xs:
            copy.wait_recv()
        total = fx[xh, xl].astype(F32)
        for i in range(3):
            total = total + xr[i].astype(F32)
        wg_out[...] = total

        for copy in grads:
            copy.wait()
        for copy in wx + qkv + wc + list(wz.values()) + list(g.values()) + pc + list(ring.values()):
            copy.wait_send()
        for copy in xs + [att_copy, d_copy]:
            copy.wait_send()

    any_space = pl.BlockSpec(memory_space=pl.ANY)
    dma = pltpu.SemaphoreType.DMA
    vmem = pltpu.VMEM
    scratch = [
        vmem((2, half, deep), BF16), vmem((2, deep, pair), BF16),
        vmem((length, cols), BF16), vmem((length, cols), BF16), vmem((length, cols), BF16),
        vmem((heads, length, length), BF16), vmem((length, length), BF16),
        vmem((heads, HEAD_DIM, length), BF16), vmem((heads, HEAD_DIM, length), BF16),
        vmem((heads, HEAD_DIM, length), BF16),
        vmem((length, cols), BF16), vmem((half, pair), BF16), vmem((length, cols), BF16),
        vmem((half, cols), BF16), vmem((half, pair), F32),
        vmem((2, NZ, 2, rows, pair), BF16), vmem((2, NZ, rows, pair), BF16),
        vmem((2, 2, NZ - 1, rows, cols), BF16), vmem((2, 2, rows, cols), BF16),
        vmem((3, rows, cols), BF16),
        vmem((length, cols), BF16), vmem((length, cols), BF16), vmem((length, cols), BF16),
        dma((32,)), dma((3,)), dma((3,)), dma((2, 2, 4)), dma((2, 2, 4)), dma((2, 8)), dma((2, 8)),
        dma((7, 3)), dma((7, 3)), dma((2, 3, NZ)), dma((2, 3, NZ)),
        dma((2,)), dma((2,)), dma((2,)), dma((2,)),
        dma((2, 2, NZ - 1)), dma((2, 2, NZ - 1)), dma((3,)), dma((3,)),
        dma((heads, 7, 3)), dma((heads, 7, 3)),
    ]
    out = jax.ShapeDtypeStruct((tokens, wide), BF16)
    return pl.pallas_call(
        kernel,
        name="joint_backward",
        out_shape=(out, out, out, jax.ShapeDtypeStruct((rows, cols), F32)),
        in_specs=[any_space] * 5,
        out_specs=(any_space, any_space, any_space, pl.BlockSpec(memory_space=pltpu.VMEM)),
        scratch_shapes=scratch,
        compiler_params=pltpu.CompilerParams(
            collective_id=0, has_side_effects=True, vmem_limit_bytes=60 * 2**20
        ),
    )


def shards(grad_out, queries, keys, values, out_weight):
    _, tokens, model = grad_out.shape
    rows, cols = out_weight.shape
    call = make_kernel(tokens, model, queries.shape[2], rows, cols, lax.axis_size("dp"))
    dq, dk, dv, wg = call(grad_out[0], queries[0], keys[0], values[0], out_weight)
    return (dq[None], dk[None], dv[None], wg)


def solution(mesh):
    in_specs = (
        P("dp", "seq", None),
        P("dp", "seq", None),
        P("dp", "seq", None),
        P("dp", "seq", None),
        P("dp", "seq"),
    )
    out_specs = (P("dp", "seq", None), P("dp", "seq", None), P("dp", "seq", None), P("dp", "seq"))
    return jax.shard_map(shards, mesh=mesh, in_specs=in_specs, out_specs=out_specs, check_vma=False)
```

```python
import math

import jax
import jax.numpy as jnp
from jax import lax
from jax.experimental import pallas as pl
from jax.experimental.pallas import tpu as pltpu
from jax.sharding import PartitionSpec as P

HEAD_DIM = 128
MESH = pl.DeviceIdType.MESH
F32 = jnp.float32
BF16 = jnp.bfloat16
NZ, NY = 8, 4
NT = (((1,), (1,)), ((), ()))
TN = (((0,), (0,)), ((), ()))


def dot(a, b):
    return jnp.dot(a, b, preferred_element_type=F32)


def make_kernel(tokens, model, wide, rows, cols, clips):
    heads = cols // HEAD_DIM
    length = tokens * 8
    half = length // 2
    strip = 2 * rows
    pair = 2 * cols
    deep = NZ * strip
    inverse_root = 1.0 / math.sqrt(HEAD_DIM)
    power = inverse_root * math.log2(math.e)
    token_scale = 1.0 / math.sqrt(clips * length)
    block = 256
    blocks = length // block

    def kernel(
        g_in, q_in, k_in, v_in, w_in,
        dq_out, dk_out, dv_out, wg_out,
        gb, wb, qb, kb, vb, pt, dsb, kt, vt, ot, att, acat, dob, dsend, dacc,
        pb, rc, rr, fx, xr, dqb, dkb, dvb,
        loc, wx_s, wx_r, wz_s, wz_r, wc_s, wc_r, qkv_s, qkv_r, g_s, g_r,
        ex_s, ex_r, pc_s, pc_r, rr_s, rr_r, x_s, x_r, gr_s, gr_r,
    ):
        dp = lax.axis_index("dp")
        seq = lax.axis_index("seq")
        z, xh, c = dp // 4, (dp // 2) % 2, dp % 2
        y, xl = seq // 2, seq % 2

        def seq_peer(dy, b):
            return {"dp": dp, "seq": ((y + dy) % NY) * 2 + (xl + b) % 2}

        def x_peer(a, b):
            return {"dp": z * 4 + ((xh + a) % 2) * 2 + c, "seq": y * 2 + (xl + b) % 2}

        def z_peer(dz):
            return {"dp": ((z + dz + NZ) % NZ) * 4 + xh * 2 + c, "seq": seq}

        core_peer = {"dp": z * 4 + xh * 2 + (1 - c), "seq": seq}
        seq_offsets = [(dy, b) for dy in range(NY) for b in range(2) if dy or b]
        x_offsets = [(0, 1), (1, 1), (1, 0)]

        def remote(src, dst, send, recv, device):
            copy = pltpu.make_async_remote_copy(
                src_ref=src, dst_ref=dst, send_sem=send, recv_sem=recv,
                device_id=device, device_id_type=MESH,
            )
            copy.start()
            return copy

        barrier = pltpu.get_barrier_semaphore()
        partners = [seq_peer(*o) for o in seq_offsets] + [core_peer, z_peer(1), z_peer(-1)]
        partners += [x_peer(1, 0), x_peer(1, 1)]
        for device in partners:
            pl.semaphore_signal(barrier, inc=1, device_id=device, device_id_type=MESH)

        def w_rows(zz, cc):
            return pl.ds(pl.multiple_of(zz * strip + cc * rows, 64), rows)

        def col(i, width):
            return pl.ds(pl.multiple_of(i * width, 128), width)

        own_rows = pl.ds(pl.multiple_of(xl * half + y * tokens, 128), tokens)
        y_rows = pl.ds(pl.multiple_of(y * tokens, 128), tokens)
        local = [
            pltpu.make_async_copy(
                w_in, wb.at[xh, w_rows(z, c), col(xl, cols)], loc.at[0]
            )
        ]
        for t, (src, dst) in enumerate(((q_in, qb), (k_in, kb), (v_in, vb))):
            local.append(
                pltpu.make_async_copy(src.at[:, col(seq, cols)], dst.at[own_rows, :], loc.at[1 + t])
            )
        for s in range(2):
            for zz in range(NZ):
                local.append(
                    pltpu.make_async_copy(
                        g_in.at[:, pl.ds((2 * zz + s) * strip, strip)],
                        gb.at[s, y_rows, pl.ds(zz * strip, strip)],
                        loc.at[4 + s * NZ + zz],
                    )
                )
        for copy in local:
            copy.start()
        pl.semaphore_wait(barrier, len(partners))

        wx = [
            remote(
                w_in, wb.at[xh, w_rows(z, c), col(xl, cols)], wx_s.at[i], wx_r.at[i], x_peer(a, b)
            )
            for i, (a, b) in enumerate(x_offsets)
        ]
        qkv = []
        for i, (dy, b) in enumerate(seq_offsets):
            device = seq_peer(dy, b)
            for t, (src, dst) in enumerate(((q_in, qb), (k_in, kb), (v_in, vb))):
                qkv.append(
                    remote(
                        src.at[:, col(device["seq"], cols)], dst.at[own_rows, :],
                        qkv_s.at[i, t], qkv_r.at[i, t], device,
                    )
                )
        for copy in local:
            copy.wait()

        wz = {}
        wc = []

        flips = [(0, 0)] + x_offsets

        def w_block(f, zz):
            a, b = flips[f]
            return wb.at[(xh + a) % 2, w_rows(zz, c), col((xl + b) % 2, cols)]

        def w_core(f, zz, slot):
            ref = w_block(f, zz)
            wc.append(remote(ref, ref, wc_s.at[f, slot], wc_r.at[f, slot], core_peer))

        def w_send(d, f, j):
            zz = (z - j + NZ) % NZ if d == 0 else (z + j) % NZ
            ref = w_block(f, zz)
            wz[d, f, j] = remote(
                ref, ref, wz_s.at[d, f, j], wz_r.at[d, f, j], z_peer(1 if d == 0 else -1)
            )

        def w_steps(d, f):
            return 4 if d == f // 2 else 3

        def w_step(j):
            for f in range(4):
                for d in range(2):
                    if j < w_steps(d, f):
                        wz[d, f, j].wait_recv()
                        if j + 1 < w_steps(d, f):
                            w_send(d, f, j + 1)
                        zz = (z - 1 - j + NZ) % NZ if d == 0 else (z + 1 + j) % NZ
                        w_core(f, zz, 1 + 2 * j + d if j < 3 else 7)

        g = {}

        def g_cols(i):
            return pl.ds(i * (deep // 2), deep // 2)

        def g_rows(dy):
            return pl.ds(pl.multiple_of(((y + dy) % NY) * tokens, 128), tokens)

        def g_copy(s, d, i, dy, slot):
            ref = gb.at[s, g_rows(dy), g_cols(i)]
            g[s, d, slot] = remote(
                ref, ref, g_s.at[s, d, slot], g_r.at[s, d, slot], seq_peer(1 if d == 0 else 3, 0)
            )

        def g_send(s):
            for slot in range(2):
                for d in range(2):
                    g_copy(s, d, slot ^ d, 0, slot)

        def g_forward(s):
            for d in range(2):
                g[s, d, 0].wait_recv()
                g_copy(s, d, d, 3 if d == 0 else 1, 2)

        def wait_g(s):
            for slot in (1, 2):
                for d in range(2):
                    g[s, d, slot].wait_recv()

        def forward(h):
            hc = pl.ds(h * HEAD_DIM, HEAD_DIM)
            kt[h] = jnp.transpose(kb[:, hc].astype(F32)).astype(BF16)
            vt[h] = jnp.transpose(vb[:, hc].astype(F32)).astype(BF16)

            @pl.loop(0, blocks)
            def _(i):
                at = pl.ds(pl.multiple_of(i * block, block), block)
                scores = lax.dot_general(kb[:, hc], qb[at, hc], NT, preferred_element_type=F32)
                largest = jnp.max(scores, axis=0, keepdims=True)
                raised = jnp.exp2((scores - largest) * power)
                total = jnp.sum(raised, axis=0, keepdims=True)
                low = (raised * (1.0 / total)).astype(BF16)
                pt[h, :, at] = low
                out = dot(vt[h], low).astype(BF16)
                ot[h, :, at] = out
                att[at, hc] = jnp.transpose(out.astype(F32)).astype(BF16)

        def project(s):
            chunk = deep // 4

            @pl.loop(0, 4)
            def _(i):
                at = pl.ds(pl.multiple_of(i * chunk, 128), chunk)
                part = dot(gb[s, :, at], wb[s, at, :])
                if s == 0:
                    dacc[...] = jnp.where(i == 0, part, dacc[...] + part)
                else:
                    dacc[...] += part

        def weight_terms(s):
            @pl.loop(0, NZ)
            def _(i):
                at = pl.ds(pl.multiple_of(i * strip, 128), strip)
                part = lax.dot_general(gb[s, :, at], acat[...], TN, preferred_element_type=F32)
                pb[s, i] = (part * token_scale).astype(BF16).reshape(2, rows, pair)

        def core_terms(s):
            return remote(pb.at[s, :, 1 - c], rc.at[s], pc_s.at[s], pc_r.at[s], core_peer)

        ring = {}
        xs = []
        for i, (a, b) in enumerate(x_offsets):
            xs.append(
                pltpu.make_async_remote_copy(
                    src_ref=fx.at[(xh + a) % 2, (xl + b) % 2], dst_ref=xr.at[i],
                    send_sem=x_s.at[i], recv_sem=x_r.at[i],
                    device_id=x_peer(a, b), device_id_type=MESH,
                )
            )

        def half_cols(q):
            return pl.ds(q * cols, cols)

        def own_terms(s, q, zd):
            return pb[s, zd, c, :, half_cols(q)].astype(F32) + rc[s, zd, :, half_cols(q)].astype(F32)

        def ring_send(s, k):
            for side in (1, 0):
                for d in range(2):
                    if k == 0 and side:
                        continue
                    zd = (z + 4 - k) % NZ if d == 0 else (z + 4 + k) % NZ
                    value = own_terms(s, d ^ side, zd)
                    if k > side:
                        ring[s, d, side, k - 1].wait_recv()
                        value = value + rr[s, d, side, k - 1].astype(F32)
                    ref = rc.at[s, zd, :, half_cols(d ^ side)]
                    ref[...] = value.astype(BF16)
                    ring[s, d, side, k] = remote(
                        ref, rr.at[s, d, side, k], rr_s.at[s, d, side, k], rr_r.at[s, d, side, k],
                        z_peer(1 if d == 0 else -1),
                    )

        def ring_last(s):
            for q in range(2):
                value = own_terms(s, q, z)
                for d in range(2):
                    ring[s, d, d ^ q, 3].wait_recv()
                    value = value + rr[s, d, d ^ q, 3].astype(F32)
                fx[s, q] = value.astype(BF16)
            for i, (a, b) in enumerate(x_offsets):

                @pl.when((xh + a) % 2 == s)
                def _():
                    xs[i].start()

        grads = []

        def backward_scores(h):
            hc = pl.ds(h * HEAD_DIM, HEAD_DIM)

            @pl.loop(0, blocks)
            def _(i):
                at = pl.ds(pl.multiple_of(i * block, block), block)
                rows_d = dob[at, hc]
                d_probs = lax.dot_general(vb[:, hc], rows_d, NT, preferred_element_type=F32)
                delta = jnp.sum(
                    jnp.transpose(rows_d.astype(F32)) * ot[h, :, at].astype(F32),
                    axis=0, keepdims=True,
                )
                low = (pt[h, :, at].astype(F32) * (d_probs - delta)).astype(BF16)
                dsb[:, at] = low
                dqb[at, hc] = jnp.transpose(dot(kt[h], low) * inverse_root).astype(BF16)

        def backward_sums(h, left, right, out, factor):
            hc = pl.ds(h * HEAD_DIM, HEAD_DIM)

            @pl.loop(0, blocks)
            def _(i):
                at = pl.ds(pl.multiple_of(i * block, block), block)
                out[at, hc] = (dot(left[at, :], right[:, hc]) * factor).astype(BF16)

        def send_grads(h, which):
            hc = pl.ds(h * HEAD_DIM, HEAD_DIM)
            out_cols = pl.ds(pl.multiple_of(seq * cols + h * HEAD_DIM, 128), HEAD_DIM)
            for t in which:
                src, dst = ((dqb, dq_out), (dkb, dk_out), (dvb, dv_out))[t]
                for i, (dy, b) in enumerate(seq_offsets):
                    token_rows = ((xl + b) % 2) * half + ((y + dy) % NY) * tokens
                    grads.append(
                        remote(
                            src.at[pl.ds(pl.multiple_of(token_rows, 128), tokens), hc],
                            dst.at[:, out_cols],
                            gr_s.at[h, i, t], gr_r.at[h, i, t], seq_peer(dy, b),
                        )
                    )
                copy = pltpu.make_async_copy(
                    src.at[own_rows, hc], dst.at[:, out_cols], loc.at[20 + h * 3 + t]
                )
                copy.start()
                grads.append(copy)

        for d in range(2):
            w_send(d, 0, 0)
        w_core(0, z, 0)
        for f in range(1, 4):
            wx[f - 1].wait_recv()
            for d in range(2):
                w_send(d, f, 0)
            w_core(f, z, 0)
        w_step(0)
        g_send(0)
        w_step(1)
        w_step(2)
        g_forward(0)
        g_send(1)
        for copy in qkv:
            copy.wait_recv()
        forward(0)
        w_step(3)
        for h in range(1, heads):
            forward(h)

        mine = pl.ds(pl.multiple_of(xl * half, 128), half)
        theirs = pl.ds(pl.multiple_of((1 - xl) * half, 128), half)
        x_partner = seq_peer(0, 1)
        att_copy = remote(
            att.at[theirs, :], acat.at[:, col(xl, cols)], ex_s.at[0], ex_r.at[0], x_partner
        )
        acat[:, col(xl, cols)] = att[mine, :]
        wait_g(0)
        att_copy.wait_recv()
        weight_terms(0)
        pc = [core_terms(0)]
        g_forward(1)
        for copy in wc:
            copy.wait_recv()
        pc[0].wait_recv()
        ring_send(0, 0)
        ring_send(0, 1)
        project(0)
        ring_send(0, 2)
        wait_g(1)
        project(1)
        d_copies = []
        for h in range(heads):
            hc = pl.ds(h * HEAD_DIM, HEAD_DIM)
            dsend[:, hc] = dacc[:, col((1 - xl) * heads + h, HEAD_DIM)].astype(BF16)
            d_copies.append(
                remote(
                    dsend.at[:, hc], dob.at[mine, hc], ex_s.at[1 + h], ex_r.at[1 + h], x_partner
                )
            )
        dob[mine, :] = dacc[:, col(xl, cols)].astype(BF16)
        ring_send(0, 3)
        weight_terms(1)
        pc.append(core_terms(1))
        d_copies[0].wait_recv()
        backward_sums(0, pt.at[0], dob, dvb, 1.0)
        send_grads(0, (2,))
        pc[1].wait_recv()
        ring_send(1, 0)
        ring_last(0)
        backward_scores(0)
        send_grads(0, (0,))
        ring_send(1, 1)
        backward_sums(0, dsb, qb, dkb, inverse_root)
        send_grads(0, (1,))
        d_copies[1].wait_recv()
        backward_sums(1, pt.at[1], dob, dvb, 1.0)
        send_grads(1, (2,))
        backward_scores(1)
        send_grads(1, (0,))
        ring_send(1, 2)
        backward_sums(1, dsb, qb, dkb, inverse_root)
        send_grads(1, (1,))
        d_copies[2].wait_recv()
        backward_sums(2, pt.at[2], dob, dvb, 1.0)
        send_grads(2, (2,))
        ring_send(1, 3)
        backward_scores(2)
        send_grads(2, (0,))
        backward_sums(2, dsb, qb, dkb, inverse_root)
        send_grads(2, (1,))
        ring_last(1)

        for copy in xs:
            copy.wait_recv()
        total = fx[xh, xl].astype(F32)
        for i in range(3):
            total = total + xr[i].astype(F32)
        wg_out[...] = total

        for copy in grads:
            copy.wait()
        for copy in wx + qkv + wc + list(wz.values()) + list(g.values()) + pc + list(ring.values()):
            copy.wait_send()
        for copy in xs + [att_copy] + d_copies:
            copy.wait_send()

    any_space = pl.BlockSpec(memory_space=pl.ANY)
    dma = pltpu.SemaphoreType.DMA
    vmem = pltpu.VMEM
    scratch = [
        vmem((2, half, deep), BF16), vmem((2, deep, pair), BF16),
        vmem((length, cols), BF16), vmem((length, cols), BF16), vmem((length, cols), BF16),
        vmem((heads, length, length), BF16), vmem((length, length), BF16),
        vmem((heads, HEAD_DIM, length), BF16), vmem((heads, HEAD_DIM, length), BF16),
        vmem((heads, HEAD_DIM, length), BF16),
        vmem((length, cols), BF16), vmem((half, pair), BF16), vmem((length, cols), BF16),
        vmem((half, cols), BF16), vmem((half, pair), F32),
        vmem((2, NZ, 2, rows, pair), BF16), vmem((2, NZ, rows, pair), BF16),
        vmem((2, 2, 2, 4, rows, cols), BF16), vmem((2, 2, rows, cols), BF16),
        vmem((3, rows, cols), BF16),
        vmem((length, cols), BF16), vmem((length, cols), BF16), vmem((length, cols), BF16),
        dma((32,)), dma((3,)), dma((3,)), dma((2, 4, 4)), dma((2, 4, 4)), dma((4, 8)), dma((4, 8)),
        dma((7, 3)), dma((7, 3)), dma((2, 2, 3)), dma((2, 2, 3)),
        dma((4,)), dma((4,)), dma((2,)), dma((2,)),
        dma((2, 2, 2, 4)), dma((2, 2, 2, 4)), dma((3,)), dma((3,)),
        dma((heads, 7, 3)), dma((heads, 7, 3)),
    ]
    out = jax.ShapeDtypeStruct((tokens, wide), BF16)
    return pl.pallas_call(
        kernel,
        name="joint_backward",
        out_shape=(out, out, out, jax.ShapeDtypeStruct((rows, cols), F32)),
        in_specs=[any_space] * 5,
        out_specs=(any_space, any_space, any_space, pl.BlockSpec(memory_space=pltpu.VMEM)),
        scratch_shapes=scratch,
        compiler_params=pltpu.CompilerParams(
            collective_id=0, has_side_effects=True, vmem_limit_bytes=60 * 2**20
        ),
    )


def shards(grad_out, queries, keys, values, out_weight):
    _, tokens, model = grad_out.shape
    rows, cols = out_weight.shape
    call = make_kernel(tokens, model, queries.shape[2], rows, cols, lax.axis_size("dp"))
    dq, dk, dv, wg = call(grad_out[0], queries[0], keys[0], values[0], out_weight)
    return (dq[None], dk[None], dv[None], wg)


def solution(mesh):
    in_specs = (
        P("dp", "seq", None),
        P("dp", "seq", None),
        P("dp", "seq", None),
        P("dp", "seq", None),
        P("dp", "seq"),
    )
    out_specs = (P("dp", "seq", None), P("dp", "seq", None), P("dp", "seq", None), P("dp", "seq"))
    return jax.shard_map(shards, mesh=mesh, in_specs=in_specs, out_specs=out_specs, check_vma=False)
```

```python
import math

import jax
import jax.numpy as jnp
from jax import lax
from jax.experimental import pallas as pl
from jax.experimental.pallas import tpu as pltpu
from jax.sharding import PartitionSpec as P

HEAD_DIM = 128
MESH = pl.DeviceIdType.MESH
F32 = jnp.float32
BF16 = jnp.bfloat16
NZ, NY = 8, 4
NT = (((1,), (1,)), ((), ()))
TN = (((0,), (0,)), ((), ()))


def dot(a, b):
    return jnp.dot(a, b, preferred_element_type=F32)


def make_kernel(tokens, model, wide, rows, cols, clips):
    heads = cols // HEAD_DIM
    length = tokens * 8
    half = length // 2
    strip = 2 * rows
    pair = 2 * cols
    deep = NZ * strip
    inverse_root = 1.0 / math.sqrt(HEAD_DIM)
    power = inverse_root * math.log2(math.e)
    token_scale = 1.0 / math.sqrt(clips * length)
    block = 256
    blocks = length // block

    def kernel(
        g_in, q_in, k_in, v_in, w_in,
        dq_out, dk_out, dv_out, wg_out,
        gb, gt, wb, qb, kb, vb, pt, dsb, kt, vt, ot, att, acat, dob, dsend, dacc,
        pb, rc, rr, fx, xr, dqb, dkb, dvb,
        loc, wx_s, wx_r, wz_s, wz_r, wc_s, wc_r, qkv_s, qkv_r, g_s, g_r,
        ex_s, ex_r, pc_s, pc_r, rr_s, rr_r, x_s, x_r, gr_s, gr_r,
    ):
        dp = lax.axis_index("dp")
        seq = lax.axis_index("seq")
        z, xh, c = dp // 4, (dp // 2) % 2, dp % 2
        y, xl = seq // 2, seq % 2

        def seq_peer(dy, b):
            return {"dp": dp, "seq": ((y + dy) % NY) * 2 + (xl + b) % 2}

        def x_peer(a, b):
            return {"dp": z * 4 + ((xh + a) % 2) * 2 + c, "seq": y * 2 + (xl + b) % 2}

        def z_peer(dz):
            return {"dp": ((z + dz + NZ) % NZ) * 4 + xh * 2 + c, "seq": seq}

        core_peer = {"dp": z * 4 + xh * 2 + (1 - c), "seq": seq}
        seq_offsets = [(dy, b) for dy in range(NY) for b in range(2) if dy or b]
        x_offsets = [(0, 1), (1, 1), (1, 0)]

        def remote(src, dst, send, recv, device):
            copy = pltpu.make_async_remote_copy(
                src_ref=src, dst_ref=dst, send_sem=send, recv_sem=recv,
                device_id=device, device_id_type=MESH,
            )
            copy.start()
            return copy

        barrier = pltpu.get_barrier_semaphore()
        partners = [seq_peer(*o) for o in seq_offsets] + [core_peer, z_peer(1), z_peer(-1)]
        partners += [x_peer(1, 0), x_peer(1, 1)]
        for device in partners:
            pl.semaphore_signal(barrier, inc=1, device_id=device, device_id_type=MESH)

        def w_rows(zz, cc):
            return pl.ds(pl.multiple_of(zz * strip + cc * rows, 64), rows)

        def col(i, width):
            return pl.ds(pl.multiple_of(i * width, 128), width)

        own_rows = pl.ds(pl.multiple_of(xl * half + y * tokens, 128), tokens)
        y_rows = pl.ds(pl.multiple_of(y * tokens, 128), tokens)
        local = [
            pltpu.make_async_copy(
                w_in, wb.at[xh, w_rows(z, c), col(xl, cols)], loc.at[0]
            )
        ]
        for t, (src, dst) in enumerate(((q_in, qb), (k_in, kb), (v_in, vb))):
            local.append(
                pltpu.make_async_copy(src.at[:, col(seq, cols)], dst.at[own_rows, :], loc.at[1 + t])
            )
        for s in range(2):
            for zz in range(NZ):
                local.append(
                    pltpu.make_async_copy(
                        g_in.at[:, pl.ds((2 * zz + s) * strip, strip)],
                        gb.at[s, y_rows, pl.ds(zz * strip, strip)],
                        loc.at[4 + s * NZ + zz],
                    )
                )
        for copy in local:
            copy.start()
        pl.semaphore_wait(barrier, len(partners))

        wx = [
            remote(
                w_in, wb.at[xh, w_rows(z, c), col(xl, cols)], wx_s.at[i], wx_r.at[i], x_peer(a, b)
            )
            for i, (a, b) in enumerate(x_offsets)
        ]
        qkv = []
        for i, (dy, b) in enumerate(seq_offsets):
            device = seq_peer(dy, b)
            for t, (src, dst) in enumerate(((q_in, qb), (k_in, kb), (v_in, vb))):
                qkv.append(
                    remote(
                        src.at[:, col(device["seq"], cols)], dst.at[own_rows, :],
                        qkv_s.at[i, t], qkv_r.at[i, t], device,
                    )
                )
        for copy in local:
            copy.wait()

        wz = {}
        wc = []

        flips = [(0, 0)] + x_offsets

        def w_block(f, zz):
            a, b = flips[f]
            return wb.at[(xh + a) % 2, w_rows(zz, c), col((xl + b) % 2, cols)]

        def w_core(f, zz, slot):
            ref = w_block(f, zz)
            wc.append(remote(ref, ref, wc_s.at[f, slot], wc_r.at[f, slot], core_peer))

        def w_send(d, f, j):
            zz = (z - j + NZ) % NZ if d == 0 else (z + j) % NZ
            ref = w_block(f, zz)
            wz[d, f, j] = remote(
                ref, ref, wz_s.at[d, f, j], wz_r.at[d, f, j], z_peer(1 if d == 0 else -1)
            )

        def w_steps(d, f):
            return 4 if d == f // 2 else 3

        def w_step(j):
            for f in range(4):
                for d in range(2):
                    if j < w_steps(d, f):
                        wz[d, f, j].wait_recv()
                        if j + 1 < w_steps(d, f):
                            w_send(d, f, j + 1)
                        zz = (z - 1 - j + NZ) % NZ if d == 0 else (z + 1 + j) % NZ
                        w_core(f, zz, 1 + 2 * j + d if j < 3 else 7)

        g = {}

        def g_cols(i):
            return pl.ds(i * (deep // 2), deep // 2)

        def g_rows(dy):
            return pl.ds(pl.multiple_of(((y + dy) % NY) * tokens, 128), tokens)

        def g_copy(s, d, i, dy, slot):
            ref = gb.at[s, g_rows(dy), g_cols(i)]
            g[s, d, slot] = remote(
                ref, ref, g_s.at[s, d, slot], g_r.at[s, d, slot], seq_peer(1 if d == 0 else 3, 0)
            )

        def g_send(s):
            for slot in range(2):
                for d in range(2):
                    g_copy(s, d, slot ^ d, 0, slot)

        def g_forward(s):
            for d in range(2):
                g[s, d, 0].wait_recv()
                g_copy(s, d, d, 3 if d == 0 else 1, 2)

        def wait_g(s, *slots):
            for slot in slots:
                for d in range(2):
                    g[s, d, slot].wait_recv()

        def forward(h):
            hc = pl.ds(h * HEAD_DIM, HEAD_DIM)
            kt[h] = jnp.transpose(kb[:, hc].astype(F32)).astype(BF16)
            vt[h] = jnp.transpose(vb[:, hc].astype(F32)).astype(BF16)

            @pl.loop(0, blocks)
            def _(i):
                at = pl.ds(pl.multiple_of(i * block, block), block)
                scores = lax.dot_general(kb[:, hc], qb[at, hc], NT, preferred_element_type=F32)
                largest = jnp.max(scores, axis=0, keepdims=True)
                raised = jnp.exp2((scores - largest) * power)
                total = jnp.sum(raised, axis=0, keepdims=True)
                low = (raised * (1.0 / total)).astype(BF16)
                pt[h, :, at] = low
                out = dot(vt[h], low).astype(BF16)
                ot[h, :, at] = out
                att[at, hc] = jnp.transpose(out.astype(F32)).astype(BF16)

        def project():
            chunk = deep // 4

            @pl.loop(0, 4)
            def _(i):
                at = pl.ds(pl.multiple_of(i * chunk, 128), chunk)
                part = dot(gb[0, :, at], wb[0, at, :])
                dacc[...] = jnp.where(i == 0, part, dacc[...] + part)

        def project_rows(*offsets):
            for dy in offsets:

                @pl.loop(0, pair // block)
                def _(i):
                    at = pl.ds(pl.multiple_of(i * block, block), block)
                    dacc[g_rows(dy), at] += dot(gb[1, g_rows(dy), :], wb[1, :, at])

        def turn_rows(*offsets):
            for dy in offsets:

                @pl.loop(0, NZ)
                def _(i):
                    at = pl.ds(pl.multiple_of(i * strip, 128), strip)
                    gt[at, g_rows(dy)] = jnp.transpose(gb[1, g_rows(dy), at])

        pc = {}

        def weight_terms(s, *offsets):
            for offset in offsets:
                zd = (z + offset) % NZ
                at = pl.ds(pl.multiple_of(zd * strip, 128), strip)
                if s == 0:
                    part = lax.dot_general(gb[0, :, at], acat[...], TN, preferred_element_type=F32)
                else:
                    part = dot(gt[at, :], acat[...])
                pb[s, zd] = (part * token_scale).astype(BF16).reshape(2, rows, pair)
                pc[s, offset] = remote(
                    pb.at[s, zd, 1 - c], rc.at[s, zd], pc_s.at[s, offset], pc_r.at[s, offset],
                    core_peer,
                )

        ring = {}
        xs = []
        for i, (a, b) in enumerate(x_offsets):
            xs.append(
                pltpu.make_async_remote_copy(
                    src_ref=fx.at[(xh + a) % 2, (xl + b) % 2], dst_ref=xr.at[i],
                    send_sem=x_s.at[i], recv_sem=x_r.at[i],
                    device_id=x_peer(a, b), device_id_type=MESH,
                )
            )

        def half_cols(q):
            return pl.ds(q * cols, cols)

        def own_terms(s, q, zd):
            return pb[s, zd, c, :, half_cols(q)].astype(F32) + rc[s, zd, :, half_cols(q)].astype(F32)

        def ring_send(s, k):
            for offset in {4 - k, 4 + k}:
                pc[s, offset].wait_recv()
            for side in (1, 0):
                for d in range(2):
                    if k == 0 and side:
                        continue
                    zd = (z + 4 - k) % NZ if d == 0 else (z + 4 + k) % NZ
                    value = own_terms(s, d ^ side, zd)
                    if k > side:
                        ring[s, d, side, k - 1].wait_recv()
                        value = value + rr[s, d, side, k - 1].astype(F32)
                    ref = rc.at[s, zd, :, half_cols(d ^ side)]
                    ref[...] = value.astype(BF16)
                    ring[s, d, side, k] = remote(
                        ref, rr.at[s, d, side, k], rr_s.at[s, d, side, k], rr_r.at[s, d, side, k],
                        z_peer(1 if d == 0 else -1),
                    )

        def ring_last(s):
            pc[s, 0].wait_recv()
            for q in range(2):
                value = own_terms(s, q, z)
                for d in range(2):
                    ring[s, d, d ^ q, 3].wait_recv()
                    value = value + rr[s, d, d ^ q, 3].astype(F32)
                fx[s, q] = value.astype(BF16)
            for i, (a, b) in enumerate(x_offsets):

                @pl.when((xh + a) % 2 == s)
                def _():
                    xs[i].start()

        grads = []

        def backward_scores(h):
            hc = pl.ds(h * HEAD_DIM, HEAD_DIM)

            @pl.loop(0, blocks)
            def _(i):
                at = pl.ds(pl.multiple_of(i * block, block), block)
                rows_d = dob[at, hc]
                d_probs = lax.dot_general(vb[:, hc], rows_d, NT, preferred_element_type=F32)
                delta = jnp.sum(
                    jnp.transpose(rows_d.astype(F32)) * ot[h, :, at].astype(F32),
                    axis=0, keepdims=True,
                )
                low = (pt[h, :, at].astype(F32) * (d_probs - delta)).astype(BF16)
                dsb[:, at] = low
                dqb[at, hc] = jnp.transpose(dot(kt[h], low) * inverse_root).astype(BF16)

        def backward_sums(h, left, right, out, factor):
            hc = pl.ds(h * HEAD_DIM, HEAD_DIM)

            out[:, hc] = (dot(left[...], right[:, hc]) * factor).astype(BF16)

        def send_grads(h, which):
            hc = pl.ds(h * HEAD_DIM, HEAD_DIM)
            out_cols = pl.ds(pl.multiple_of(seq * cols + h * HEAD_DIM, 128), HEAD_DIM)
            for t in which:
                src, dst = ((dqb, dq_out), (dkb, dk_out), (dvb, dv_out))[t]
                for i, (dy, b) in enumerate(seq_offsets):
                    token_rows = ((xl + b) % 2) * half + ((y + dy) % NY) * tokens
                    grads.append(
                        remote(
                            src.at[pl.ds(pl.multiple_of(token_rows, 128), tokens), hc],
                            dst.at[:, out_cols],
                            gr_s.at[h, i, t], gr_r.at[h, i, t], seq_peer(dy, b),
                        )
                    )
                copy = pltpu.make_async_copy(
                    src.at[own_rows, hc], dst.at[:, out_cols], loc.at[20 + h * 3 + t]
                )
                copy.start()
                grads.append(copy)

        g_send(0)
        for d in range(2):
            w_send(d, 0, 0)
        w_core(0, z, 0)
        for f in range(1, 4):
            wx[f - 1].wait_recv()
            for d in range(2):
                w_send(d, f, 0)
            w_core(f, z, 0)
        mine = pl.ds(pl.multiple_of(xl * half, 128), half)
        theirs = pl.ds(pl.multiple_of((1 - xl) * half, 128), half)
        x_partner = seq_peer(0, 1)
        att_copies = []

        def send_attended(h):
            hc = pl.ds(h * HEAD_DIM, HEAD_DIM)
            ac = col(xl * heads + h, HEAD_DIM)
            att_copies.append(
                remote(att.at[theirs, hc], acat.at[:, ac], ex_s.at[h], ex_r.at[h], x_partner)
            )
            acat[:, ac] = att[mine, hc]

        d_copies = []

        def send_d_attn():
            for h in range(heads):
                hc = pl.ds(h * HEAD_DIM, HEAD_DIM)
                dsend[:, hc] = dacc[:, col((1 - xl) * heads + h, HEAD_DIM)].astype(BF16)
                d_copies.append(
                    remote(
                        dsend.at[:, hc], dob.at[mine, hc],
                        ex_s.at[heads + h], ex_r.at[heads + h], x_partner,
                    )
                )
            dob[mine, :] = dacc[:, col(xl, cols)].astype(BF16)

        w_step(0)
        w_step(1)
        g_forward(0)
        for copy in qkv:
            copy.wait_recv()
        forward(0)
        send_attended(0)
        w_step(2)
        g_send(1)
        forward(1)
        send_attended(1)
        forward(2)
        send_attended(2)
        wait_g(0, 1, 2)
        for copy in att_copies:
            copy.wait_recv()
        weight_terms(0, 4, 3, 5)
        ring_send(0, 0)
        weight_terms(0, 2, 6, 1, 7, 0)
        ring_send(0, 1)
        g_forward(1)
        w_step(3)
        for copy in wc:
            copy.wait_recv()
        project()
        turn_rows(0)
        project_rows(0)
        ring_send(0, 2)
        wait_g(1, 1)
        turn_rows(1, 3)
        project_rows(1, 3)
        wait_g(1, 2)
        project_rows(2)
        send_d_attn()
        turn_rows(2)
        weight_terms(1, 4, 3, 5)
        ring_send(0, 3)
        ring_send(1, 0)
        d_copies[0].wait_recv()
        backward_sums(0, pt.at[0], dob, dvb, 1.0)
        send_grads(0, (2,))
        d_copies[1].wait_recv()
        backward_sums(1, pt.at[1], dob, dvb, 1.0)
        send_grads(1, (2,))
        weight_terms(1, 2, 6)
        d_copies[2].wait_recv()
        backward_sums(2, pt.at[2], dob, dvb, 1.0)
        send_grads(2, (2,))
        ring_send(1, 1)
        ring_last(0)
        backward_scores(0)
        send_grads(0, (0,))
        weight_terms(1, 1, 7, 0)
        backward_sums(0, dsb, qb, dkb, inverse_root)
        send_grads(0, (1,))
        ring_send(1, 2)
        backward_scores(1)
        send_grads(1, (0,))
        backward_sums(1, dsb, qb, dkb, inverse_root)
        send_grads(1, (1,))
        ring_send(1, 3)
        backward_scores(2)
        send_grads(2, (0,))
        backward_sums(2, dsb, qb, dkb, inverse_root)
        send_grads(2, (1,))
        ring_last(1)

        for copy in xs:
            copy.wait_recv()
        total = fx[xh, xl].astype(F32)
        for i in range(3):
            total = total + xr[i].astype(F32)
        wg_out[...] = total

        for copy in grads:
            copy.wait()
        for copy in wx + qkv + wc + list(wz.values()) + list(g.values()) + list(ring.values()):
            copy.wait_send()
        for copy in xs + att_copies + d_copies + list(pc.values()):
            copy.wait_send()

    any_space = pl.BlockSpec(memory_space=pl.ANY)
    dma = pltpu.SemaphoreType.DMA
    vmem = pltpu.VMEM
    scratch = [
        vmem((2, half, deep), BF16), vmem((deep, half), BF16), vmem((2, deep, pair), BF16),
        vmem((length, cols), BF16), vmem((length, cols), BF16), vmem((length, cols), BF16),
        vmem((heads, length, length), BF16), vmem((length, length), BF16),
        vmem((heads, HEAD_DIM, length), BF16), vmem((heads, HEAD_DIM, length), BF16),
        vmem((heads, HEAD_DIM, length), BF16),
        vmem((length, cols), BF16), vmem((half, pair), BF16), vmem((length, cols), BF16),
        vmem((half, cols), BF16), vmem((half, pair), F32),
        vmem((2, NZ, 2, rows, pair), BF16), vmem((2, NZ, rows, pair), BF16),
        vmem((2, 2, 2, 4, rows, cols), BF16), vmem((2, 2, rows, cols), BF16),
        vmem((3, rows, cols), BF16),
        vmem((length, cols), BF16), vmem((length, cols), BF16), vmem((length, cols), BF16),
        dma((32,)), dma((3,)), dma((3,)), dma((2, 4, 4)), dma((2, 4, 4)), dma((4, 8)), dma((4, 8)),
        dma((7, 3)), dma((7, 3)), dma((2, 2, 3)), dma((2, 2, 3)),
        dma((2 * heads,)), dma((2 * heads,)), dma((2, NZ)), dma((2, NZ)),
        dma((2, 2, 2, 4)), dma((2, 2, 2, 4)), dma((3,)), dma((3,)),
        dma((heads, 7, 3)), dma((heads, 7, 3)),
    ]
    out = jax.ShapeDtypeStruct((tokens, wide), BF16)
    return pl.pallas_call(
        kernel,
        name="joint_backward",
        out_shape=(out, out, out, jax.ShapeDtypeStruct((rows, cols), F32)),
        in_specs=[any_space] * 5,
        out_specs=(any_space, any_space, any_space, pl.BlockSpec(memory_space=pltpu.VMEM)),
        scratch_shapes=scratch,
        compiler_params=pltpu.CompilerParams(
            collective_id=0, has_side_effects=True, vmem_limit_bytes=60 * 2**20
        ),
    )


def place(arrays):
    count = len(arrays)

    def kernel(*refs):
        sources, targets, held = refs[:count], refs[count : 2 * count], refs[2 * count : 3 * count]
        sems = refs[3 * count]
        loads = [pltpu.make_async_copy(sources[i], held[i], sems.at[0, i]) for i in range(count)]
        stores = [pltpu.make_async_copy(held[i], targets[i], sems.at[1, i]) for i in range(count)]
        for copy in loads:
            copy.start()
        for load, store in zip(loads, stores):
            load.wait()
            store.start()
        for copy in stores:
            copy.wait()

    any_space = pl.BlockSpec(memory_space=pl.ANY)
    return pl.pallas_call(
        kernel,
        name="place",
        out_shape=tuple(jax.ShapeDtypeStruct(a.shape, a.dtype) for a in arrays),
        in_specs=[any_space] * count,
        out_specs=(any_space,) * count,
        scratch_shapes=[pltpu.VMEM(a.shape, a.dtype) for a in arrays]
        + [pltpu.SemaphoreType.DMA((2, count))],
    )(*arrays)


def shards(grad_out, queries, keys, values, out_weight):
    _, tokens, model = grad_out.shape
    rows, cols = out_weight.shape
    call = make_kernel(tokens, model, queries.shape[2], rows, cols, lax.axis_size("dp"))
    results = call(grad_out[0], queries[0], keys[0], values[0], out_weight)
    dq, dk, dv, wg = place(results)
    return (dq[None], dk[None], dv[None], wg)


def solution(mesh):
    in_specs = (
        P("dp", "seq", None),
        P("dp", "seq", None),
        P("dp", "seq", None),
        P("dp", "seq", None),
        P("dp", "seq"),
    )
    out_specs = (P("dp", "seq", None), P("dp", "seq", None), P("dp", "seq", None), P("dp", "seq"))
    return jax.shard_map(shards, mesh=mesh, in_specs=in_specs, out_specs=out_specs, check_vma=False)
```

```python
import math

import jax
import jax.numpy as jnp
from jax import lax
from jax.experimental import pallas as pl
from jax.experimental.pallas import tpu as pltpu
from jax.sharding import PartitionSpec as P

HEAD_DIM = 128
MESH = pl.DeviceIdType.MESH
F32 = jnp.float32
BF16 = jnp.bfloat16
NZ, NY = 8, 4
NT = (((1,), (1,)), ((), ()))
TN = (((0,), (0,)), ((), ()))


def dot(a, b):
    return jnp.dot(a, b, preferred_element_type=F32)


def make_kernel(tokens, model, wide, rows, cols, clips):
    heads = cols // HEAD_DIM
    length = tokens * 8
    half = length // 2
    strip = 2 * rows
    pair = 2 * cols
    deep = NZ * strip
    inverse_root = 1.0 / math.sqrt(HEAD_DIM)
    power = inverse_root * math.log2(math.e)
    token_scale = 1.0 / math.sqrt(clips * length)
    block = 256
    blocks = length // block

    def kernel(
        g_in, q_in, k_in, v_in, w_in,
        dq_out, dk_out, dv_out, wg_out,
        gb, gt, wb, qb, kb, vb, pt, dsb, kt, vt, ot, att, acat, dob, dsend, dacc,
        pb, rc, rr, fx, xr, dqb, dkb, dvb,
        loc, wx_s, wx_r, wz_s, wz_r, wc_s, wc_r, qkv_s, qkv_r, g_s, g_r,
        ex_s, ex_r, pc_s, pc_r, rr_s, rr_r, x_s, x_r, gr_s, gr_r,
    ):
        dp = lax.axis_index("dp")
        seq = lax.axis_index("seq")
        z, xh, c = dp // 4, (dp // 2) % 2, dp % 2
        y, xl = seq // 2, seq % 2

        def seq_peer(dy, b):
            return {"dp": dp, "seq": ((y + dy) % NY) * 2 + (xl + b) % 2}

        def core_turn(dy):
            return dy + c * (NY - 2 * dy)

        def x_peer(a, b):
            return {"dp": z * 4 + ((xh + a) % 2) * 2 + c, "seq": y * 2 + (xl + b) % 2}

        def z_peer(dz):
            return {"dp": ((z + dz + NZ) % NZ) * 4 + xh * 2 + c, "seq": seq}

        core_peer = {"dp": z * 4 + xh * 2 + (1 - c), "seq": seq}
        seq_offsets = [(dy, b) for dy in range(NY) for b in range(2) if dy or b]
        x_offsets = [(0, 1), (1, 1), (1, 0)]

        def remote(src, dst, send, recv, device):
            copy = pltpu.make_async_remote_copy(
                src_ref=src, dst_ref=dst, send_sem=send, recv_sem=recv,
                device_id=device, device_id_type=MESH,
            )
            copy.start()
            return copy

        barrier = pltpu.get_barrier_semaphore()
        partners = [seq_peer(*o) for o in seq_offsets] + [core_peer, z_peer(1), z_peer(-1)]
        partners += [x_peer(1, 0), x_peer(1, 1)]
        for device in partners:
            pl.semaphore_signal(barrier, inc=1, device_id=device, device_id_type=MESH)

        def w_rows(zz, cc):
            return pl.ds(pl.multiple_of(zz * strip + cc * rows, 64), rows)

        def col(i, width):
            return pl.ds(pl.multiple_of(i * width, 128), width)

        own_rows = pl.ds(pl.multiple_of(xl * half + y * tokens, 128), tokens)
        y_rows = pl.ds(pl.multiple_of(y * tokens, 128), tokens)
        local = [
            pltpu.make_async_copy(
                w_in, wb.at[xh, w_rows(z, c), col(xl, cols)], loc.at[0]
            )
        ]
        for t, (src, dst) in enumerate(((q_in, qb), (k_in, kb), (v_in, vb))):
            local.append(
                pltpu.make_async_copy(src.at[:, col(seq, cols)], dst.at[own_rows, :], loc.at[1 + t])
            )
        for s in range(2):
            for zz in range(NZ):
                local.append(
                    pltpu.make_async_copy(
                        g_in.at[:, pl.ds((2 * zz + s) * strip, strip)],
                        gb.at[s, y_rows, pl.ds(zz * strip, strip)],
                        loc.at[4 + s * NZ + zz],
                    )
                )
        for copy in local:
            copy.start()
        pl.semaphore_wait(barrier, len(partners))

        wx = [
            remote(
                w_in, wb.at[xh, w_rows(z, c), col(xl, cols)], wx_s.at[i], wx_r.at[i], x_peer(a, b)
            )
            for i, (a, b) in enumerate(x_offsets)
        ]
        qkv = []
        for i, (dy, b) in enumerate(seq_offsets):
            device = seq_peer(core_turn(dy), b)
            for t, (src, dst) in enumerate(((q_in, qb), (k_in, kb), (v_in, vb))):
                qkv.append(
                    remote(
                        src.at[:, col(device["seq"], cols)], dst.at[own_rows, :],
                        qkv_s.at[i, t], qkv_r.at[i, t], device,
                    )
                )
        for copy in local:
            copy.wait()

        wz = {}
        wc = []

        flips = [(0, 0)] + x_offsets

        def w_block(f, zz):
            a, b = flips[f]
            return wb.at[(xh + a) % 2, w_rows(zz, c), col((xl + b) % 2, cols)]

        def w_core(f, zz, slot):
            ref = w_block(f, zz)
            wc.append(remote(ref, ref, wc_s.at[f, slot], wc_r.at[f, slot], core_peer))

        def w_send(d, f, j):
            zz = (z - j + NZ) % NZ if d == 0 else (z + j) % NZ
            ref = w_block(f, zz)
            wz[d, f, j] = remote(
                ref, ref, wz_s.at[d, f, j], wz_r.at[d, f, j], z_peer(1 if d == 0 else -1)
            )

        def w_steps(d, f):
            return 4 if d == f // 2 else 3

        def w_step(j):
            for f in range(4):
                for d in range(2):
                    if j < w_steps(d, f):
                        wz[d, f, j].wait_recv()
                        if j + 1 < w_steps(d, f):
                            w_send(d, f, j + 1)
                        zz = (z - 1 - j + NZ) % NZ if d == 0 else (z + 1 + j) % NZ
                        w_core(f, zz, 1 + 2 * j + d if j < 3 else 7)

        g = {}

        def g_cols(i):
            return pl.ds(i * (deep // 2), deep // 2)

        def g_rows(dy):
            return pl.ds(pl.multiple_of(((y + dy) % NY) * tokens, 128), tokens)

        def g_copy(s, d, i, dy, slot):
            ref = gb.at[s, g_rows(dy), g_cols(i)]
            g[s, d, slot] = remote(
                ref, ref, g_s.at[s, d, slot], g_r.at[s, d, slot], seq_peer(1 if d == 0 else 3, 0)
            )

        def g_send(s):
            for slot in range(2):
                for d in range(2):
                    g_copy(s, d, slot ^ d, 0, slot)

        def g_forward(s):
            for d in range(2):
                g[s, d, 0].wait_recv()
                g_copy(s, d, d, 3 if d == 0 else 1, 2)

        def wait_g(s, *slots):
            for slot in slots:
                for d in range(2):
                    g[s, d, slot].wait_recv()

        def forward(h):
            hc = pl.ds(h * HEAD_DIM, HEAD_DIM)
            kt[h] = jnp.transpose(kb[:, hc].astype(F32)).astype(BF16)
            vt[h] = jnp.transpose(vb[:, hc].astype(F32)).astype(BF16)

            @pl.loop(0, blocks)
            def _(i):
                at = pl.ds(pl.multiple_of(i * block, block), block)
                scores = lax.dot_general(kb[:, hc], qb[at, hc], NT, preferred_element_type=F32)
                largest = jnp.max(scores, axis=0, keepdims=True)
                raised = jnp.exp2((scores - largest) * power)
                total = jnp.sum(raised, axis=0, keepdims=True)
                low = (raised * (1.0 / total)).astype(BF16)
                pt[h, :, at] = low
                out = dot(vt[h], low).astype(BF16)
                ot[h, :, at] = out
                att[at, hc] = jnp.transpose(out.astype(F32)).astype(BF16)

        def project():
            chunk = deep // 4

            @pl.loop(0, 4)
            def _(i):
                at = pl.ds(pl.multiple_of(i * chunk, 128), chunk)
                part = dot(gb[0, :, at], wb[0, at, :])
                dacc[...] = jnp.where(i == 0, part, dacc[...] + part)

        def project_rows(*offsets):
            for dy in offsets:

                @pl.loop(0, pair // block)
                def _(i):
                    at = pl.ds(pl.multiple_of(i * block, block), block)
                    dacc[g_rows(dy), at] += dot(gb[1, g_rows(dy), :], wb[1, :, at])

        def turn_rows(*offsets):
            for dy in offsets:

                @pl.loop(0, NZ)
                def _(i):
                    at = pl.ds(pl.multiple_of(i * strip, 128), strip)
                    gt[at, g_rows(dy)] = jnp.transpose(gb[1, g_rows(dy), at])

        pc = {}

        def weight_terms(s, *offsets):
            for offset in offsets:
                zd = (z + offset) % NZ
                at = pl.ds(pl.multiple_of(zd * strip, 128), strip)
                if s == 0:
                    part = lax.dot_general(gb[0, :, at], acat[...], TN, preferred_element_type=F32)
                else:
                    part = dot(gt[at, :], acat[...])
                pb[s, zd] = (part * token_scale).astype(BF16).reshape(2, rows, pair)
                pc[s, offset] = remote(
                    pb.at[s, zd, 1 - c], rc.at[s, zd], pc_s.at[s, offset], pc_r.at[s, offset],
                    core_peer,
                )

        ring = {}
        xs = []
        for i, (a, b) in enumerate(x_offsets):
            xs.append(
                pltpu.make_async_remote_copy(
                    src_ref=fx.at[(xh + a) % 2, (xl + b) % 2], dst_ref=xr.at[i],
                    send_sem=x_s.at[i], recv_sem=x_r.at[i],
                    device_id=x_peer(a, b), device_id_type=MESH,
                )
            )

        def half_cols(q):
            return pl.ds(q * cols, cols)

        def own_terms(s, q, zd):
            return pb[s, zd, c, :, half_cols(q)].astype(F32) + rc[s, zd, :, half_cols(q)].astype(F32)

        def ring_send(s, k):
            for offset in {4 - k, 4 + k}:
                pc[s, offset].wait_recv()
            for side in (1, 0):
                for d in range(2):
                    if k == 0 and side:
                        continue
                    zd = (z + 4 - k) % NZ if d == 0 else (z + 4 + k) % NZ
                    value = own_terms(s, d ^ side, zd)
                    if k > side:
                        ring[s, d, side, k - 1].wait_recv()
                        value = value + rr[s, d, side, k - 1].astype(F32)
                    ref = rc.at[s, zd, :, half_cols(d ^ side)]
                    ref[...] = value.astype(BF16)
                    ring[s, d, side, k] = remote(
                        ref, rr.at[s, d, side, k], rr_s.at[s, d, side, k], rr_r.at[s, d, side, k],
                        z_peer(1 if d == 0 else -1),
                    )

        def ring_last(s):
            pc[s, 0].wait_recv()
            for q in range(2):
                value = own_terms(s, q, z)
                for d in range(2):
                    ring[s, d, d ^ q, 3].wait_recv()
                    value = value + rr[s, d, d ^ q, 3].astype(F32)
                fx[s, q] = value.astype(BF16)
            for i, (a, b) in enumerate(x_offsets):

                @pl.when((xh + a) % 2 == s)
                def _():
                    xs[i].start()

        grads = []

        def backward_scores(h):
            hc = pl.ds(h * HEAD_DIM, HEAD_DIM)

            @pl.loop(0, blocks)
            def _(i):
                at = pl.ds(pl.multiple_of(i * block, block), block)
                rows_d = dob[at, hc]
                d_probs = lax.dot_general(vb[:, hc], rows_d, NT, preferred_element_type=F32)
                delta = jnp.sum(
                    jnp.transpose(rows_d.astype(F32)) * ot[h, :, at].astype(F32),
                    axis=0, keepdims=True,
                )
                low = (pt[h, :, at].astype(F32) * (d_probs - delta)).astype(BF16)
                dsb[:, at] = low
                dqb[at, hc] = jnp.transpose(dot(kt[h], low) * inverse_root).astype(BF16)

        def backward_sums(h, left, right, out, factor):
            hc = pl.ds(h * HEAD_DIM, HEAD_DIM)

            out[:, hc] = (dot(left[...], right[:, hc]) * factor).astype(BF16)

        def send_grads(h, which):
            hc = pl.ds(h * HEAD_DIM, HEAD_DIM)
            out_cols = pl.ds(pl.multiple_of(seq * cols + h * HEAD_DIM, 128), HEAD_DIM)
            for t in which:
                src, dst = ((dqb, dq_out), (dkb, dk_out), (dvb, dv_out))[t]
                for i, (dy, b) in enumerate(seq_offsets):
                    token_rows = ((xl + b) % 2) * half + ((y + core_turn(dy)) % NY) * tokens
                    grads.append(
                        remote(
                            src.at[pl.ds(pl.multiple_of(token_rows, 128), tokens), hc],
                            dst.at[:, out_cols],
                            gr_s.at[h, i, t], gr_r.at[h, i, t], seq_peer(core_turn(dy), b),
                        )
                    )
                copy = pltpu.make_async_copy(
                    src.at[own_rows, hc], dst.at[:, out_cols], loc.at[20 + h * 3 + t]
                )
                copy.start()
                grads.append(copy)

        g_send(0)
        for d in range(2):
            w_send(d, 0, 0)
        w_core(0, z, 0)
        for f in range(1, 4):
            wx[f - 1].wait_recv()
            for d in range(2):
                w_send(d, f, 0)
            w_core(f, z, 0)
        mine = pl.ds(pl.multiple_of(xl * half, 128), half)
        theirs = pl.ds(pl.multiple_of((1 - xl) * half, 128), half)
        x_partner = seq_peer(0, 1)
        att_copies = []

        def send_attended(h):
            hc = pl.ds(h * HEAD_DIM, HEAD_DIM)
            ac = col(xl * heads + h, HEAD_DIM)
            att_copies.append(
                remote(att.at[theirs, hc], acat.at[:, ac], ex_s.at[h], ex_r.at[h], x_partner)
            )
            acat[:, ac] = att[mine, hc]

        d_copies = []

        def send_d_attn():
            for h in range(heads):
                hc = pl.ds(h * HEAD_DIM, HEAD_DIM)
                dsend[:, hc] = dacc[:, col((1 - xl) * heads + h, HEAD_DIM)].astype(BF16)
                d_copies.append(
                    remote(
                        dsend.at[:, hc], dob.at[mine, hc],
                        ex_s.at[heads + h], ex_r.at[heads + h], x_partner,
                    )
                )
            dob[mine, :] = dacc[:, col(xl, cols)].astype(BF16)

        w_step(0)
        w_step(1)
        g_forward(0)
        for copy in qkv:
            copy.wait_recv()
        forward(0)
        send_attended(0)
        w_step(2)
        g_send(1)
        forward(1)
        send_attended(1)
        forward(2)
        send_attended(2)
        wait_g(0, 1, 2)
        for copy in att_copies:
            copy.wait_recv()
        weight_terms(0, 4, 3, 5)
        ring_send(0, 0)
        weight_terms(0, 2, 6, 1, 7, 0)
        ring_send(0, 1)
        g_forward(1)
        w_step(3)
        for copy in wc:
            copy.wait_recv()
        project()
        turn_rows(0)
        project_rows(0)
        ring_send(0, 2)
        wait_g(1, 1)
        turn_rows(1, 3)
        project_rows(1, 3)
        wait_g(1, 2)
        project_rows(2)
        send_d_attn()
        turn_rows(2)
        weight_terms(1, 4, 3, 5)
        ring_send(0, 3)
        ring_send(1, 0)
        d_copies[0].wait_recv()
        backward_sums(0, pt.at[0], dob, dvb, 1.0)
        send_grads(0, (2,))
        d_copies[1].wait_recv()
        backward_sums(1, pt.at[1], dob, dvb, 1.0)
        send_grads(1, (2,))
        weight_terms(1, 2, 6)
        d_copies[2].wait_recv()
        backward_sums(2, pt.at[2], dob, dvb, 1.0)
        send_grads(2, (2,))
        ring_send(1, 1)
        ring_last(0)
        backward_scores(0)
        send_grads(0, (0,))
        weight_terms(1, 1, 7, 0)
        backward_sums(0, dsb, qb, dkb, inverse_root)
        send_grads(0, (1,))
        ring_send(1, 2)
        backward_scores(1)
        send_grads(1, (0,))
        backward_sums(1, dsb, qb, dkb, inverse_root)
        send_grads(1, (1,))
        ring_send(1, 3)
        backward_scores(2)
        send_grads(2, (0,))
        backward_sums(2, dsb, qb, dkb, inverse_root)
        send_grads(2, (1,))
        ring_last(1)

        for copy in xs:
            copy.wait_recv()
        total = fx[xh, xl].astype(F32)
        for i in range(3):
            total = total + xr[i].astype(F32)
        wg_out[...] = total

        for copy in grads:
            copy.wait()
        for copy in wx + qkv + wc + list(wz.values()) + list(g.values()) + list(ring.values()):
            copy.wait_send()
        for copy in xs + att_copies + d_copies + list(pc.values()):
            copy.wait_send()

    any_space = pl.BlockSpec(memory_space=pl.ANY)
    dma = pltpu.SemaphoreType.DMA
    vmem = pltpu.VMEM
    scratch = [
        vmem((2, half, deep), BF16), vmem((deep, half), BF16), vmem((2, deep, pair), BF16),
        vmem((length, cols), BF16), vmem((length, cols), BF16), vmem((length, cols), BF16),
        vmem((heads, length, length), BF16), vmem((length, length), BF16),
        vmem((heads, HEAD_DIM, length), BF16), vmem((heads, HEAD_DIM, length), BF16),
        vmem((heads, HEAD_DIM, length), BF16),
        vmem((length, cols), BF16), vmem((half, pair), BF16), vmem((length, cols), BF16),
        vmem((half, cols), BF16), vmem((half, pair), F32),
        vmem((2, NZ, 2, rows, pair), BF16), vmem((2, NZ, rows, pair), BF16),
        vmem((2, 2, 2, 4, rows, cols), BF16), vmem((2, 2, rows, cols), BF16),
        vmem((3, rows, cols), BF16),
        vmem((length, cols), BF16), vmem((length, cols), BF16), vmem((length, cols), BF16),
        dma((32,)), dma((3,)), dma((3,)), dma((2, 4, 4)), dma((2, 4, 4)), dma((4, 8)), dma((4, 8)),
        dma((7, 3)), dma((7, 3)), dma((2, 2, 3)), dma((2, 2, 3)),
        dma((2 * heads,)), dma((2 * heads,)), dma((2, NZ)), dma((2, NZ)),
        dma((2, 2, 2, 4)), dma((2, 2, 2, 4)), dma((3,)), dma((3,)),
        dma((heads, 7, 3)), dma((heads, 7, 3)),
    ]
    out = jax.ShapeDtypeStruct((tokens, wide), BF16)
    return pl.pallas_call(
        kernel,
        name="joint_backward",
        out_shape=(out, out, out, jax.ShapeDtypeStruct((rows, cols), F32)),
        in_specs=[any_space] * 5,
        out_specs=(any_space, any_space, any_space, pl.BlockSpec(memory_space=pltpu.VMEM)),
        scratch_shapes=scratch,
        compiler_params=pltpu.CompilerParams(
            collective_id=0, has_side_effects=True, vmem_limit_bytes=60 * 2**20
        ),
    )


def place(arrays):
    count = len(arrays)

    def kernel(*refs):
        sources, targets, held = refs[:count], refs[count : 2 * count], refs[2 * count : 3 * count]
        sems = refs[3 * count]
        loads = [pltpu.make_async_copy(sources[i], held[i], sems.at[0, i]) for i in range(count)]
        stores = [pltpu.make_async_copy(held[i], targets[i], sems.at[1, i]) for i in range(count)]
        for copy in loads:
            copy.start()
        for load, store in zip(loads, stores):
            load.wait()
            store.start()
        for copy in stores:
            copy.wait()

    any_space = pl.BlockSpec(memory_space=pl.ANY)
    return pl.pallas_call(
        kernel,
        name="place",
        out_shape=tuple(jax.ShapeDtypeStruct(a.shape, a.dtype) for a in arrays),
        in_specs=[any_space] * count,
        out_specs=(any_space,) * count,
        scratch_shapes=[pltpu.VMEM(a.shape, a.dtype) for a in arrays]
        + [pltpu.SemaphoreType.DMA((2, count))],
    )(*arrays)


def shards(grad_out, queries, keys, values, out_weight):
    _, tokens, model = grad_out.shape
    rows, cols = out_weight.shape
    call = make_kernel(tokens, model, queries.shape[2], rows, cols, lax.axis_size("dp"))
    results = call(grad_out[0], queries[0], keys[0], values[0], out_weight)
    dq, dk, dv, wg = place(results)
    return (dq[None], dk[None], dv[None], wg)


def solution(mesh):
    in_specs = (
        P("dp", "seq", None),
        P("dp", "seq", None),
        P("dp", "seq", None),
        P("dp", "seq", None),
        P("dp", "seq"),
    )
    out_specs = (P("dp", "seq", None), P("dp", "seq", None), P("dp", "seq", None), P("dp", "seq"))
    return jax.shard_map(shards, mesh=mesh, in_specs=in_specs, out_specs=out_specs, check_vma=False)
```
